32 devices in a mesh: groups: 2 (over x), blk: 16 (over z, y, core).
Axes of the slice: x: 2, y: 2, z: 4, core: 2. Of those that a mesh axis runs over, the one named last changes fastest.
Arguments:
- item_rows: bfloat16 [16384, 1024], P(('groups', 'blk')), parts along dimension 0, may hold values from -6 to 6
- item_slot: int32 [16384], P('groups'), parts along dimension 0, may hold values from 0 to 8191, as said below
- w_up: bfloat16 [1024, 2048], replicated, may hold values from -0.1875 to 0.1875
- w_down: bfloat16 [2048, 1024], replicated, may hold values from -0.125 to 0.125
- events: bfloat16 [2048, 1024], P(('groups', 'blk')), parts along dimension 0, may hold values from -6 to 6
- w_query: bfloat16 [1024, 1024], replicated, may hold values from -0.1875 to 0.1875
- history_kv: bfloat16 [2048, 2, 1024], P(('groups', 'blk')), parts along dimension 0, may hold values from -6 to 6
- window_start: int32 [2048], P(('groups', 'blk')), parts along dimension 0, may hold values from 0 to 1023, as said below
- cand: int32 [2048, 16], P(('groups', 'blk')), parts along dimension 0, may hold values from 0 to 8191, as said below
- cand_count: int32 [2048], P(('groups', 'blk')), parts along dimension 0, may hold values from 1 to 16
Outputs:
- item_out: bfloat16 [16384, 1024], P(('groups', 'blk')), parts along dimension 0
- scores: float32 [2048, 16], P(('groups', 'blk')), parts along dimension 0
The draws below stay inside these ranges and needn't reach their ends.
There are 2 independent parts, one for each index of `groups`. The reference program is written for one: setup_inputs(seed, part) draws one part's arguments, and reference() takes and returns one part's arrays. A program takes and returns all parts, laid end to end along the dimension named above; an argument that names none is the same for every part. Nothing has to cross between parts.
Inputs may be any that keep to these rules, and one draw needn't show every extreme that they name: A permutation of the item ids; item id m lies on the owner item_slot[m] // 512. `cand`: of the 1024 slots of one device, at most 128 name items of one owner; some owner is named by exactly 128 slots of every device. window_start[i] <= i and i - window_start[i] < 512; i - window_start[i] = 511 for some event.
All inputs are finite; a program needn't handle non-finite values.
Results may differ from the reference program's by a relative error of at most 0.0067.
Values may be sent and summed in bfloat16 or wider, within the bound.
No kernel may reach another device: no remote copies, remote signals or barrier semaphores. Data moves between devices by JAX's collectives and lax.ppermute only.
A program may use at most 128 MiB of HBM per device.

```python
import jax
import jax.numpy as jnp
from jax import lax

D = 1024
HID = 2048
HEADS = 8
HD = 128
ATT = 1024
WIN = 512
CAND = 16
HIST_DEV = 64
ITEM_DEV = 512
CAP = 128
N_EVENTS = 1024
ITEMS = 8192


def owner_table(key):
    return jax.random.permutation(jax.random.fold_in(key, 11), ITEMS)


def draw_item_slot(key, part):
    return owner_table(key).astype(jnp.int32)


def draw_cand(key, part):
    block_count = N_EVENTS // HIST_DEV
    slot_count = HIST_DEV * CAND
    store_slot = owner_table(key).astype(jnp.int32)
    item_of_slot = jnp.argsort(store_slot).astype(jnp.int32)
    hot_owner = jax.random.randint(jax.random.fold_in(key, 12), (), 0, block_count).astype(jnp.int32)
    rest_keys = jax.random.split(jax.random.fold_in(key, 13), block_count)
    rest_pos = jax.vmap(lambda one_key: jax.random.permutation(one_key, (block_count - 1) * CAP))(rest_keys)
    rest_owner = (rest_pos[:, :slot_count - CAP] // CAP).astype(jnp.int32)
    rest_owner = rest_owner + (rest_owner >= hot_owner).astype(jnp.int32)
    hot_part = jnp.zeros((block_count, CAP), jnp.int32) + hot_owner
    owner_rows = jnp.concatenate([hot_part, rest_owner], axis=1)
    shuffle_keys = jax.random.split(jax.random.fold_in(key, 14), block_count)
    shuffle_rows = jax.vmap(lambda one_key: jax.random.permutation(one_key, slot_count))(shuffle_keys)
    owner_rows = jnp.take_along_axis(owner_rows, shuffle_rows, axis=1)
    local_rows = jax.random.randint(jax.random.fold_in(key, 15), (block_count, slot_count), 0, ITEM_DEV).astype(jnp.int32)
    item_ids = item_of_slot[owner_rows * ITEM_DEV + local_rows]
    return item_ids.reshape(N_EVENTS, CAND).astype(jnp.int32)


def draw_window_start(key, part):
    positions = jnp.arange(N_EVENTS, dtype=jnp.int32)
    spans = jax.random.randint(jax.random.fold_in(key, 21), (N_EVENTS,), 1, WIN + 1).astype(jnp.int32)
    full_row = jax.random.randint(jax.random.fold_in(key, 22), (N_EVENTS // HIST_DEV,), 0, HIST_DEV).astype(jnp.int32)
    is_full = positions % HIST_DEV == jnp.repeat(full_row, HIST_DEV)
    spans = jnp.where(is_full, WIN, spans)
    return jnp.maximum(positions - spans + 1, 0).astype(jnp.int32)


def set_ends(result, key, low, top_value):
    dims = result.shape
    index_at = [jax.random.randint(jax.random.fold_in(key, axis), (), 0, dims[axis]) for axis in range(len(dims))]
    result = result.at[tuple(index_at)].set(low)
    longest = dims.index(max(dims))
    index_at[longest] = (index_at[longest] + 1) % dims[longest]
    return result.at[tuple(index_at)].set(top_value)


def steps_of(own_key, shape, cuts, low, largest):
    def one(axis_at, blocks):
        heights = jax.random.uniform(jax.random.fold_in(jax.random.fold_in(own_key, 6), axis_at), (blocks,), jnp.float32, low / len(cuts), largest / len(cuts))
        return jnp.repeat(jnp.exp(heights), shape[axis_at] // blocks).reshape((-1,) + (1,) * (len(shape) - axis_at - 1))

    loudness = one(*cuts[0])
    for cut in cuts[1:]:
        loudness = loudness * one(*cut)
    return loudness


def noise(key, shape, scale, most, shards=(), kind=jnp.bfloat16):
    array = scale * jax.random.normal(key, shape, jnp.float32)
    if shards:
        array = array * steps_of(key, shape, shards, -0.22, 0.18)
    return jnp.clip(array, -most, most).astype(kind)


def setup_inputs(seed: int = 0, part: int = 0) -> dict:
    key_list = jax.random.split(jax.random.key(seed), 11)
    part_keys = jax.random.split(jax.random.fold_in(key_list[10], part), 11)
    return {
        "item_rows": noise(part_keys[0], (ITEMS, D), 1.0, 6.0, ((0, 16),)),
        "item_slot": draw_item_slot(jax.random.fold_in(jax.random.fold_in(key_list[10], part), 71), part),
        "w_up": noise(key_list[2], (D, HID), D ** -0.5, 0.1875),
        "w_down": noise(key_list[3], (HID, D), HID ** -0.5, 0.125),
        "events": noise(part_keys[4], (N_EVENTS, D), 1.0, 6.0, ((0, 16),)),
        "w_query": noise(key_list[5], (D, ATT), D ** -0.5, 0.1875),
        "history_kv": noise(part_keys[6], (N_EVENTS, 2, ATT), 1.0, 6.0, ((0, 16),)),
        "window_start": draw_window_start(jax.random.fold_in(jax.random.fold_in(key_list[10], part), 71), part),
        "cand": draw_cand(jax.random.fold_in(jax.random.fold_in(key_list[10], part), 71), part),
        "cand_count": set_ends(jax.random.randint(part_keys[9], (N_EVENTS,), 1, CAND + 1), jax.random.fold_in(part_keys[9], 1), 1, CAND).astype(jnp.int32),
    }


def reference(item_rows, item_slot, w_up, w_down, events, w_query, history_kv, window_start, cand, cand_count):
    hidden = jax.nn.silu(jnp.dot(item_rows, w_up, preferred_element_type=jnp.float32)).astype(jnp.bfloat16)
    item_out = (item_rows.astype(jnp.float32) + jnp.dot(hidden, w_down, preferred_element_type=jnp.float32)).astype(jnp.bfloat16)
    queries = jnp.dot(events, w_query, preferred_element_type=jnp.float32).astype(jnp.bfloat16)
    queries = queries.reshape(N_EVENTS, HEADS, HD)
    padding = WIN - HIST_DEV
    padded_kv = jnp.concatenate([jnp.zeros((padding, 2, ATT), jnp.bfloat16), history_kv], axis=0)
    score_scale = HD ** -0.5

    def one_block(block_index):
        first_pos = (block_index * HIST_DEV).astype(jnp.int32)
        query_rows = lax.dynamic_slice_in_dim(queries, first_pos, HIST_DEV, 0).astype(jnp.float32)
        kv_rows = lax.dynamic_slice_in_dim(padded_kv, first_pos, WIN, 0)
        starts = lax.dynamic_slice_in_dim(window_start, first_pos, HIST_DEV, 0)
        query_pos = first_pos + jnp.arange(HIST_DEV, dtype=jnp.int32)
        key_pos = first_pos - padding + jnp.arange(WIN, dtype=jnp.int32)
        inside = ((key_pos[None, :] <= query_pos[:, None]) & (key_pos[None, :] >= starts[:, None])).astype(jnp.float32)
        key_rows = kv_rows[:, 0].reshape(WIN, HEADS, HD).astype(jnp.float32)
        value_rows = kv_rows[:, 1].reshape(WIN, HEADS, HD).astype(jnp.float32)
        logits = jnp.einsum("qhd,khd->hqk", query_rows, key_rows) * score_scale
        weights = (jax.nn.silu(logits) * inside[None] / WIN).astype(jnp.bfloat16)
        weights = lax.optimization_barrier(weights).astype(jnp.float32)
        mixed = jnp.einsum("hqk,khd->qhd", weights, value_rows)
        return mixed.reshape(HIST_DEV, ATT)

    attended = lax.map(one_block, jnp.arange(N_EVENTS // HIST_DEV, dtype=jnp.int32))
    user = attended.reshape(N_EVENTS, ATT).astype(jnp.bfloat16)
    store_slot = item_slot[cand]
    picked = item_out[store_slot]
    raw_scores = jnp.einsum("ecd,ed->ec", picked.astype(jnp.float32), user.astype(jnp.float32))
    live_mask = jnp.arange(CAND, dtype=jnp.int32)[None, :] < cand_count[:, None]
    scores = jnp.where(live_mask, raw_scores, jnp.float32(0.0))
    return item_out, scores
```

```python
import functools

import jax
import jax.numpy as jnp
from jax import lax
from jax.experimental import pallas as pl
from jax.experimental.pallas import tpu as pltpu
from jax.sharding import PartitionSpec as P

HEADS = 8
WIN = 512
PLANE = 4
LANES = 128

VMEM_SPEC = pl.BlockSpec(memory_space=pltpu.VMEM)
PARAMS = pltpu.CompilerParams(vmem_limit_bytes=48 * 1024 * 1024)


def call(body, out_shape, args, scratch=(), flops=0, name=None):
    size = sum(a.size * a.dtype.itemsize for a in args)
    return pl.pallas_call(
        body,
        out_shape=out_shape,
        in_specs=[VMEM_SPEC] * len(args),
        out_specs=jax.tree.map(lambda _: VMEM_SPEC, out_shape),
        scratch_shapes=list(scratch),
        compiler_params=PARAMS,
        cost_estimate=pl.CostEstimate(flops=flops, bytes_accessed=size, transcendentals=0),
        name=name,
    )(*args)


def in_plane(value, step):
    count = lax.axis_size("blk")
    pairs = [(s, (s // PLANE) * PLANE + ((s % PLANE) ^ step)) for s in range(count)]
    return lax.ppermute(value, "blk", pairs)


def along(value, step, wrap):
    count = lax.axis_size("blk")
    shift = step * PLANE
    if wrap:
        pairs = [(s, (s + shift) % count) for s in range(count)]
    else:
        pairs = [(s, s + shift) for s in range(count - shift)]
    return lax.ppermute(value, "blk", pairs)


def my_place():
    index = lax.axis_index("blk")
    return index // PLANE, index % PLANE


def kv_pieces_kernel(kv_ref, *rest):
    outs, (key_buf, value_buf) = rest[:PLANE], rest[PLANE:]
    part = outs[0].shape[1] // 2
    column = my_place()[1]
    key_buf[...] = kv_ref[:, 0, :]
    value_buf[...] = kv_ref[:, 1, :]
    for step in range(PLANE):
        window = pl.ds(pl.multiple_of((column ^ step) * part, part), part)
        outs[step][:, :part] = key_buf[:, window]
        outs[step][:, part:] = value_buf[:, window]


def query_kernel(hist_rows, event_ref, weight_ref, cand_ref, table_ref, start_ref, *rest):
    outs, query_buf = rest[:PLANE], rest[PLANE]
    part = outs[0].shape[1]
    index = lax.axis_index("blk")
    column = index % PLANE
    slots = cand_ref.shape[0]
    query_buf[...] = jnp.dot(
        event_ref[...], weight_ref[...], preferred_element_type=jnp.float32
    ).astype(jnp.bfloat16)
    ids = cand_ref[...]
    ids = jnp.concatenate([ids, ids], axis=1)
    table_row = ids // LANES
    table_lane = ids % LANES

    def look(row, found):
        values = jnp.broadcast_to(table_ref[pl.ds(row, 1), :], ids.shape)
        picked = jnp.take_along_axis(values, table_lane, axis=1)
        return jnp.where(table_row == row, picked, found)

    slot = lax.fori_loop(0, table_ref.shape[0], look, jnp.zeros_like(ids), unroll=8)
    first_half = lax.broadcasted_iota(jnp.int32, ids.shape, 1) < hist_rows
    slot_meta = jnp.where(first_half, slot // 256, slot % 256)
    starts = start_ref[...]
    starts = jnp.concatenate([starts, starts], axis=1)
    place = index * hist_rows + lax.broadcasted_iota(jnp.int32, starts.shape, 1) % hist_rows
    reach = index * hist_rows + hist_rows - WIN
    offset = place - jnp.maximum(starts, reach)
    offset = jnp.broadcast_to(offset, ids.shape)
    offset_meta = jnp.where(first_half, offset // 16, offset % 16)
    meta = jnp.concatenate([slot_meta, offset_meta], axis=1)
    meta = meta.astype(jnp.float32).astype(jnp.bfloat16)
    for step in range(PLANE):
        window = pl.ds(pl.multiple_of((column ^ step) * part, part), part)
        outs[step][:hist_rows, :] = query_buf[:, window]
        outs[step][hist_rows:, :] = meta


def attend_kernel(hist_rows, shifts, *refs):
    queries = refs[:PLANE]
    blocks = refs[PLANE : PLANE + shifts + 1]
    out_ref = refs[PLANE + shifts + 1]
    plane, column = my_place()
    part = queries[0].shape[1]
    rows = PLANE * hist_rows
    head_size = out_ref.shape[1] * PLANE // HEADS
    heads = part // head_size
    scale = head_size**-0.5

    def positions(shape, axis, shift):
        at = lax.broadcasted_iota(jnp.int32, shape, axis)
        return ((plane - shift) * PLANE + (column ^ (at // hist_rows))) * hist_rows + at % hist_rows

    offsets = []
    for step in range(PLANE):
        meta = queries[step][hist_rows:, LANES:].astype(jnp.float32)
        offset = meta[:, :hist_rows] * 16 + meta[:, hist_rows:]
        offsets.append(jnp.transpose(offset)[:, :1])
    offset = jnp.concatenate(offsets, axis=0).astype(jnp.int32)
    query_pos = positions((rows, 1), 0, 0)
    starts = query_pos - offset
    query = jnp.concatenate([queries[step][:hist_rows, :] for step in range(PLANE)], axis=0)
    insides = []
    for shift in range(shifts + 1):
        key_pos = positions((1, rows), 1, shift)
        insides.append((key_pos <= query_pos) & (key_pos >= starts))
    for head in range(heads):
        window = slice(head * head_size, (head + 1) * head_size)
        total = jnp.zeros((rows, head_size), jnp.float32)
        for shift in range(shifts + 1):
            key = blocks[shift][:, window]
            value = blocks[shift][:, part + head * head_size : part + (head + 1) * head_size]
            logits = (
                lax.dot_general(
                    query[:, window],
                    key,
                    (((1,), (1,)), ((), ())),
                    preferred_element_type=jnp.float32,
                )
                * scale
            )
            weights = jnp.where(insides[shift], jax.nn.silu(logits) * (1.0 / WIN), 0.0)
            total += jnp.dot(
                weights.astype(jnp.bfloat16), value, preferred_element_type=jnp.float32
            )
        out_ref[:rows, window] = total.astype(jnp.bfloat16)
    slots = queries[0].shape[0] - hist_rows
    for step in range(PLANE):
        row, lane = divmod(step * LANES, part)
        out_ref[rows + row * slots : rows + (row + 1) * slots, lane : lane + LANES] = queries[step][
            hist_rows:, :LANES
        ]


def score_kernel(hist_rows, first, ordered, *refs):
    count = len(refs) - PLANE - 1
    users, items, out_ref = refs[:count], refs[count : count + PLANE], refs[-1]
    plane, column = my_place()
    planes = lax.axis_size("blk") // PLANE
    rows = PLANE * hist_rows
    part = items[0].shape[1]
    store_rows = items[0].shape[0]
    slots = out_ref.shape[1]
    ids = []
    for user in users:
        pieces = []
        for step in range(PLANE):
            row, lane = divmod(step * LANES, part)
            meta = user[rows + row * slots : rows + (row + 1) * slots, lane : lane + LANES]
            meta = meta.astype(jnp.float32)
            pieces.append(meta[:, :hist_rows] * 256 + meta[:, hist_rows:])
        ids.append(jnp.concatenate(pieces, axis=1))
    pad = LANES - count * slots
    if pad:
        ids.append(jnp.zeros((pad, rows), jnp.float32))
    local = jnp.transpose(jnp.concatenate(ids, axis=0)).astype(jnp.int32)
    local = local - plane * (PLANE * store_rows)
    owned = (local >= 0) & (local < PLANE * store_rows)
    place = ((local // store_rows) ^ column) * store_rows + local % store_rows
    lane_of = lax.broadcasted_iota(jnp.int32, local.shape, 1) // slots
    chunk_of = jnp.where(owned, place // LANES, -1)
    lane_at = place & (LANES - 1)
    total = jnp.zeros(local.shape, jnp.float32)
    for at, user in enumerate(users):
        mine = jnp.where(lane_of == at, chunk_of, -1)
        for step in range(PLANE):
            dense = lax.dot_general(
                user[:rows, :],
                items[step][...],
                (((1,), (1,)), ((), ())),
                preferred_element_type=jnp.float32,
            )
            for chunk in range(store_rows // LANES):
                picked = jnp.take_along_axis(
                    dense[:, chunk * LANES : (chunk + 1) * LANES], lane_at, axis=1
                )
                here = mine == step * (store_rows // LANES) + chunk
                total = jnp.where(here, picked, total)
    turned = jnp.transpose(total)
    for at in range(count):
        for step in range(PLANE):
            block = turned[at * slots : (at + 1) * slots, step * hist_rows : (step + 1) * hist_rows]
            if ordered:
                to_plane = lax.rem(plane + planes - (first + at), planes)
                out_ref[to_plane * PLANE + (column ^ step)] = block
            else:
                out_ref[at * PLANE + (column ^ step)] = block


def per_device(
    item_rows, item_slot, w_up, w_down, events, w_query, history_kv, window_start, cand, cand_count
):
    block_count = lax.axis_size("blk")
    planes = block_count // PLANE
    plane, column = my_place()
    hist_rows = events.shape[0]
    store_rows, width = item_rows.shape
    cand_slots = cand.shape[1]
    att = history_kv.shape[2]
    part = att // PLANE
    rows = PLANE * hist_rows
    bf16 = jnp.bfloat16

    kv_own = call(
        kv_pieces_kernel,
        [jax.ShapeDtypeStruct((hist_rows, 2 * part), bf16)] * PLANE,
        [history_kv],
        [pltpu.VMEM((hist_rows, att), bf16)] * 2,
        name="kv_pieces",
    )
    kv_plane = [kv_own[0]] + [in_plane(kv_own[step], step) for step in range(1, PLANE)]
    query_own = call(
        functools.partial(query_kernel, hist_rows),
        [jax.ShapeDtypeStruct((hist_rows + cand_slots, part), bf16)] * PLANE,
        [
            events,
            w_query,
            cand.T,
            item_slot.reshape(-1, LANES),
            window_start.reshape(1, -1),
        ],
        [pltpu.VMEM((hist_rows, att), bf16)],
        flops=2 * hist_rows * width * att,
        name="query_pieces",
    )
    query_plane = [query_own[0]] + [in_plane(query_own[step], step) for step in range(1, PLANE)]
    kv_block = jnp.concatenate(kv_plane, axis=0)
    shifts = -(-(WIN // hist_rows - 1) // PLANE)
    kv_blocks = [kv_block] + [along(kv_block, step, False) for step in range(1, shifts + 1)]

    hidden = jax.nn.silu(jnp.dot(item_rows, w_up, preferred_element_type=jnp.float32)).astype(bf16)
    item_out = (
        item_rows.astype(jnp.float32) + jnp.dot(hidden, w_down, preferred_element_type=jnp.float32)
    ).astype(bf16)
    item_parts = [
        lax.dynamic_slice_in_dim(item_out, (column ^ step) * part, part, 1) for step in range(PLANE)
    ]
    item_plane = [item_parts[0]] + [in_plane(item_parts[step], step) for step in range(1, PLANE)]

    user = call(
        functools.partial(attend_kernel, hist_rows, shifts),
        jax.ShapeDtypeStruct((rows + PLANE * cand_slots * LANES // part, part), bf16),
        query_plane + kv_blocks,
        flops=4 * rows * rows * (shifts + 1) * part,
        name="attend",
    )
    users = [user] + [along(user, step, True) for step in range(1, planes)]
    together = min(planes, LANES // cand_slots, 4)
    results = []
    for first in range(0, planes, together):
        results.append(
            call(
                functools.partial(score_kernel, hist_rows, first, planes == together),
                jax.ShapeDtypeStruct((together * PLANE, cand_slots, hist_rows), jnp.float32),
                users[first : first + together] + item_plane,
                flops=2 * together * rows * part * PLANE * store_rows,
                name="scores",
            )
        )
    if len(results) == 1:
        partial = results[0]
    else:
        order = (plane - jnp.arange(planes, dtype=jnp.int32)) % planes
        partial = jnp.concatenate(results).reshape(planes, PLANE, cand_slots, hist_rows)
        partial = partial[order].reshape(block_count, cand_slots, hist_rows)
    gathered = lax.all_to_all(partial, "blk", split_axis=0, concat_axis=0, tiled=True)
    raw_scores = jnp.sum(gathered, axis=0)
    live_mask = jnp.arange(cand_slots, dtype=jnp.int32)[:, None] < cand_count[None, :]
    scores = jnp.where(live_mask, raw_scores, jnp.float32(0.0)).T
    return (item_out, scores)


def solution(mesh):
    in_specs = (
        P(("groups", "blk"), None),
        P("groups"),
        P(),
        P(),
        P(("groups", "blk"), None),
        P(),
        P(("groups", "blk"), None, None),
        P(("groups", "blk")),
        P(("groups", "blk"), None),
        P(("groups", "blk")),
    )
    out_specs = (P(("groups", "blk"), None), P(("groups", "blk"), None))
    return jax.shard_map(
        per_device, mesh=mesh, in_specs=in_specs, out_specs=out_specs, check_vma=False
    )
```

```python
import functools

import jax
import jax.numpy as jnp
from jax import lax
from jax.experimental import pallas as pl
from jax.experimental.pallas import tpu as pltpu
from jax.sharding import PartitionSpec as P


HEADS = 8
WIN = 512
PLANE = 4
LANES = 128
TILE = 512

VMEM_SPEC = pl.BlockSpec(memory_space=pltpu.VMEM)
HBM_SPEC = pl.BlockSpec(memory_space=pltpu.MemorySpace.HBM)
VMEM_LIMIT = 24 * 1024 * 1024
QUERY_GRANT = 66_400_000
MLP_GRANT = 62_000_000


def call(body, out_shape, args, scratch=(), flops=0, grant=None, first_out=None):
    size = sum(a.size * a.dtype.itemsize for a in args)
    out_specs = jax.tree.map(lambda _: VMEM_SPEC, out_shape)
    if first_out is not None:
        out_specs[0] = first_out
    return pl.pallas_call(
        body,
        out_shape=out_shape,
        in_specs=[HBM_SPEC if grant else VMEM_SPEC] * len(args),
        out_specs=out_specs,
        scratch_shapes=list(scratch),
        compiler_params=pltpu.CompilerParams(vmem_limit_bytes=grant or VMEM_LIMIT),
        cost_estimate=pl.CostEstimate(flops=flops, bytes_accessed=size, transcendentals=0),
    )(*args)


def in_plane(value, step):
    count = lax.axis_size("blk")
    pairs = [(s, (s // PLANE) * PLANE + ((s % PLANE) ^ step)) for s in range(count)]
    return lax.ppermute(value, "blk", pairs)


def forward(value, step):
    count = lax.axis_size("blk")
    return lax.ppermute(value, "blk", [(s, (s + step * PLANE) % count) for s in range(count)])


def swap(value, step):
    count = lax.axis_size("blk")
    return lax.ppermute(value, "blk", [(s, s ^ (step * PLANE)) for s in range(count)])


def my_place():
    index = lax.axis_index("blk")
    return index // PLANE, index % PLANE


def part_windows(part):
    column = my_place()[1]
    return [pl.ds(pl.multiple_of((column ^ step) * part, part), part) for step in range(PLANE)]


def copies_of(pairs, sems):
    return [
        pltpu.make_async_copy(source, target, sems.at[at])
        for at, (source, target) in enumerate(pairs)
    ]


def kv_pieces_kernel(kv_ref, *rest):
    outs, (key_buf, value_buf) = rest[:PLANE], rest[PLANE:]
    part = outs[0].shape[1] // 2
    windows = part_windows(part)
    key_buf[...] = kv_ref[:, 0, :]
    value_buf[...] = kv_ref[:, 1, :]
    for step in range(PLANE):
        outs[step][:, :part] = key_buf[:, windows[step]]
        outs[step][:, part:] = value_buf[:, windows[step]]


def query_kernel(event_hbm, weight_hbm, cand_hbm, table_hbm, start_hbm, *rest):
    query_outs, rest = rest[:PLANE], rest[PLANE:]
    event_ref, weight_ref, cand_ref, table_ref, start_ref, query_buf, sems = rest
    index = lax.axis_index("blk")
    hist_rows = event_ref.shape[0]
    part = query_outs[0].shape[1]
    windows = part_windows(part)
    copies = copies_of(
        [
            (cand_hbm, cand_ref),
            (table_hbm, table_ref),
            (start_hbm, start_ref),
            (event_hbm, event_ref),
            (weight_hbm, weight_ref),
        ],
        sems,
    )
    for copy in copies:
        copy.start()
    for copy in copies[:3]:
        copy.wait()
    ids = cand_ref[...]
    ids = jnp.concatenate([ids, ids], axis=1)
    table_row = ids // LANES
    table_lane = ids % LANES

    def look(row, found):
        values = jnp.broadcast_to(table_ref[pl.ds(row, 1), :], ids.shape)
        picked = jnp.take_along_axis(values, table_lane, axis=1, mode="promise_in_bounds")
        return jnp.where(table_row == row, picked, found)

    slot = lax.fori_loop(0, table_ref.shape[0], look, jnp.zeros_like(ids), unroll=8)
    first_half = lax.broadcasted_iota(jnp.int32, ids.shape, 1) < hist_rows
    slot_meta = jnp.where(first_half, slot // 256, slot % 256)
    starts = start_ref[...]
    starts = jnp.concatenate([starts, starts], axis=1)
    place = index * hist_rows + lax.broadcasted_iota(jnp.int32, starts.shape, 1) % hist_rows
    reach = index * hist_rows + hist_rows - WIN
    offset = place - jnp.maximum(starts, reach)
    offset = jnp.broadcast_to(offset, ids.shape)
    offset_meta = jnp.where(first_half, offset // 16, offset % 16)
    meta = jnp.concatenate([slot_meta, offset_meta], axis=1)
    meta = meta.astype(jnp.float32).astype(jnp.bfloat16)
    for copy in copies[3:]:
        copy.wait()
    query = jnp.dot(event_ref[...], weight_ref[...], preferred_element_type=jnp.float32)
    query_buf[...] = query.astype(jnp.bfloat16)
    for step in range(PLANE):
        query_outs[step][:hist_rows, :] = query_buf[:, windows[step]]
        query_outs[step][hist_rows:, :] = meta


def join_kernel(*refs):
    pieces, (all_ref, late_ref) = refs[:PLANE], refs[PLANE:]
    column = my_place()[1]
    rows = pieces[0].shape[0]
    for step in range(PLANE):
        all_ref[step * rows : (step + 1) * rows, :] = pieces[step][...]
    for block in range(1, PLANE):
        start = pl.multiple_of((column ^ block) * rows, rows)
        late_ref[(block - 1) * rows : block * rows, :] = all_ref[pl.ds(start, rows), :]


def collect_kernel(hist_rows, *refs):
    out_ref = refs[-1]
    slots = refs[0].shape[0] - hist_rows
    for step in range(PLANE):
        out_ref[step * slots : (step + 1) * slots, :] = refs[step][hist_rows:, :LANES]


def attend_kernel(hist_rows, shifts, *refs):
    queries, out_ref = refs[:PLANE], refs[-1]
    blocks = refs[PLANE:-1]
    plane, column = my_place()
    part = queries[0].shape[1]
    rows = PLANE * hist_rows
    head_size = out_ref.shape[1] * PLANE // HEADS
    heads = part // head_size
    scale = head_size**-0.5

    def positions(shape, axis, shift):
        at = lax.broadcasted_iota(jnp.int32, shape, axis)
        full = shape[axis] == rows
        block = (column ^ (at // hist_rows)) if full else 1 + at // hist_rows
        return ((plane - shift) * PLANE + block) * hist_rows + at % hist_rows

    offsets = []
    for step in range(PLANE):
        meta = queries[step][hist_rows:, LANES:].astype(jnp.float32)
        offset = meta[:, :hist_rows] * 16 + meta[:, hist_rows:]
        offsets.append(jnp.transpose(offset)[:, :1])
    offset = jnp.concatenate(offsets, axis=0).astype(jnp.int32)
    query_pos = positions((rows, 1), 0, 0)
    starts = query_pos - offset
    query = jnp.concatenate([queries[step][:hist_rows, :] for step in range(PLANE)], axis=0)
    totals = [jnp.zeros((rows, head_size), jnp.float32) for _ in range(heads)]
    for shift in range(shifts + 1):
        keys = blocks[shift][...]
        key_pos = positions((1, keys.shape[0]), 1, shift)
        inside = (key_pos <= query_pos) & (key_pos >= starts)
        for head in range(heads):
            window = slice(head * head_size, (head + 1) * head_size)
            logits = scale * lax.dot_general(
                query[:, window],
                keys[:, window],
                (((1,), (1,)), ((), ())),
                preferred_element_type=jnp.float32,
            )
            weights = jnp.where(inside, jax.nn.silu(logits) * (1.0 / WIN), 0.0)
            totals[head] += jnp.dot(
                weights.astype(jnp.bfloat16),
                keys[:, part + head * head_size : part + (head + 1) * head_size],
                preferred_element_type=jnp.float32,
            )
    for head in range(heads):
        window = slice(head * head_size, (head + 1) * head_size)
        out_ref[:, window] = totals[head].astype(jnp.bfloat16)


def mlp_kernel(row_hbm, up_hbm, down_hbm, out_hbm, *rest):
    parts, (row_ref, up_ref, down_ref, hidden_ref, sems) = rest[:PLANE], rest[PLANE:]
    windows = part_windows(parts[0].shape[1])
    hidden_size = up_ref.shape[1]
    half = hidden_size // 2
    quarter = hidden_size // 4
    loads = [(row_hbm, row_ref)]
    loads += [(up_hbm.at[:, w], up_ref.at[:, w]) for w in (slice(0, half), slice(half, None))]
    loads += [
        (down_hbm.at[pl.ds(at * quarter, quarter)], down_ref.at[pl.ds(at * quarter, quarter)])
        for at in range(4)
    ]
    saves = [(parts[step], out_hbm.at[:, windows[step]]) for step in range(PLANE)]
    copies = copies_of(loads + saves, sems)
    for copy in copies[:7]:
        copy.start()
    copies[0].wait()
    for at in range(0, hidden_size, TILE):
        if at % half == 0:
            copies[1 + at // half].wait()
        hidden = jnp.dot(
            row_ref[...], up_ref[:, at : at + TILE], preferred_element_type=jnp.float32
        )
        hidden_ref[:, at : at + TILE] = jax.nn.silu(hidden).astype(jnp.bfloat16)
    for copy in copies[3:7]:
        copy.wait()
    for step in range(PLANE):
        mixed = jnp.dot(
            hidden_ref[...], down_ref[:, windows[step]], preferred_element_type=jnp.float32
        )
        mixed = row_ref[:, windows[step]].astype(jnp.float32) + mixed
        parts[step][...] = mixed.astype(jnp.bfloat16)
        copies[7 + step].start()
    for copy in copies[7:]:
        copy.wait()


def place_kernel(hist_rows, store_rows, *refs):
    metas, out_ref = refs[:-1], refs[-1]
    plane, column = my_place()
    slots = metas[0].shape[0] // PLANE
    ids = []
    for meta_ref in metas:
        pieces = []
        for step in range(PLANE):
            meta = meta_ref[step * slots : (step + 1) * slots, :].astype(jnp.float32)
            pieces.append(meta[:, :hist_rows] * 256 + meta[:, hist_rows:])
        ids.append(jnp.concatenate(pieces, axis=1))
    pad = LANES - len(metas) * slots
    if pad:
        ids.append(jnp.zeros((pad, PLANE * hist_rows), jnp.float32))
    local = jnp.transpose(jnp.concatenate(ids, axis=0)).astype(jnp.int32)
    local = local - plane * (PLANE * store_rows)
    owned = (local >= 0) & (local < PLANE * store_rows)
    place = ((local // store_rows) ^ column) * store_rows + local % store_rows
    out_ref[...] = jnp.where(owned, place, -1)


def score_kernel(hist_rows, slots, at, first, *refs):
    user_ref, items, place_ref = refs[0], refs[1 : 1 + PLANE], refs[1 + PLANE]
    before_ref = None if first else refs[2 + PLANE]
    out_ref, dense_ref = refs[-2:]
    store_rows = items[0].shape[0]
    for step in range(PLANE):
        dense_ref[:, step * store_rows : (step + 1) * store_rows] = lax.dot_general(
            user_ref[...],
            items[step][...],
            (((1,), (1,)), ((), ())),
            preferred_element_type=jnp.float32,
        )
    for tile in range(PLANE):
        rows = slice(tile * hist_rows, (tile + 1) * hist_rows)
        place = place_ref[rows, :]
        lane_at = place & (LANES - 1)
        lane_of = lax.broadcasted_iota(jnp.int32, place.shape, 1) // slots
        mine = jnp.where((lane_of == at) & (place >= 0), place // LANES, -1)
        total = jnp.zeros(place.shape, jnp.float32) if first else before_ref[rows, :]
        for chunk in range(PLANE * store_rows // LANES):
            picked = jnp.take_along_axis(
                dense_ref[rows, chunk * LANES : (chunk + 1) * LANES],
                lane_at,
                axis=1,
                mode="promise_in_bounds",
            )
            total = jnp.where(mine == chunk, picked, total)
        out_ref[rows, :] = total


def send_kernel(hist_rows, slots, ordered, total_ref, out_ref):
    plane, column = my_place()
    turned = jnp.transpose(total_ref[...])
    half = slots // 2
    for at in range(out_ref.shape[0] // PLANE):
        for step in range(PLANE):
            lanes = slice(step * hist_rows, (step + 1) * hist_rows)
            block = jnp.concatenate(
                [
                    turned[at * slots : at * slots + half, lanes],
                    turned[at * slots + half : (at + 1) * slots, lanes],
                ],
                axis=1,
            )
            to_plane = plane ^ at if ordered else at
            out_ref[to_plane * PLANE + (column ^ step)] = block


def finish_kernel(part_ref, count_ref, out_ref):
    total = part_ref[0]
    for at in range(1, part_ref.shape[0]):
        total = total + part_ref[at]
    hist_rows = out_ref.shape[1]
    total = jnp.concatenate([total[:, :hist_rows], total[:, hist_rows:]], axis=0)
    live = lax.broadcasted_iota(jnp.int32, total.shape, 0) < count_ref[...]
    out_ref[...] = jnp.where(live, total, 0.0)


def per_device(
    item_rows, item_slot, w_up, w_down, events, w_query, history_kv, window_start, cand, cand_count
):
    block_count = lax.axis_size("blk")
    planes = block_count // PLANE
    plane, _ = my_place()
    hist_rows = events.shape[0]
    store_rows, width = item_rows.shape
    hidden_size = w_up.shape[1]
    cand_slots = cand.shape[1]
    att = history_kv.shape[2]
    part = att // PLANE
    rows = PLANE * hist_rows
    bf16 = jnp.bfloat16
    reach = WIN // hist_rows - 1
    shifts = -(-reach // PLANE)
    steps = range(1, PLANE)

    kv_own = call(
        kv_pieces_kernel,
        [jax.ShapeDtypeStruct((hist_rows, 2 * part), bf16)] * PLANE,
        [history_kv],
        [pltpu.VMEM((hist_rows, att), bf16)] * 2,
    )
    kv_plane = [kv_own[0]] + [in_plane(kv_own[step], step) for step in steps]
    query_own = call(
        query_kernel,
        [jax.ShapeDtypeStruct((hist_rows + cand_slots, part), bf16)] * PLANE,
        [events, w_query, cand.T, item_slot.reshape(-1, LANES), window_start.reshape(1, -1)],
        [
            pltpu.VMEM(events.shape, bf16),
            pltpu.VMEM(w_query.shape, bf16),
            pltpu.VMEM((cand_slots, hist_rows), jnp.int32),
            pltpu.VMEM((item_slot.shape[0] // LANES, LANES), jnp.int32),
            pltpu.VMEM((1, hist_rows), jnp.int32),
            pltpu.VMEM((hist_rows, att), bf16),
            pltpu.SemaphoreType.DMA((5,)),
        ],
        flops=2 * hist_rows * width * att,
        grant=QUERY_GRANT,
    )
    query_plane = [query_own[0]] + [in_plane(query_own[step], step) for step in steps]
    kv_all, kv_late = call(
        join_kernel,
        [
            jax.ShapeDtypeStruct((rows, 2 * part), bf16),
            jax.ShapeDtypeStruct((rows - hist_rows, 2 * part), bf16),
        ],
        kv_plane,
    )
    kv_blocks = [kv_all] + [
        forward(kv_late if shift * PLANE > reach else kv_all, shift)
        for shift in range(1, shifts + 1)
    ]

    meta = call(
        functools.partial(collect_kernel, hist_rows),
        jax.ShapeDtypeStruct((PLANE * cand_slots, LANES), bf16),
        query_plane,
    )
    metas = [meta] + [swap(meta, step) for step in range(1, planes)]

    mlp = call(
        mlp_kernel,
        [jax.ShapeDtypeStruct((store_rows, width), bf16)]
        + [jax.ShapeDtypeStruct((store_rows, part), bf16)] * PLANE,
        [item_rows, w_up, w_down],
        [
            pltpu.VMEM((store_rows, width), bf16),
            pltpu.VMEM((width, hidden_size), bf16),
            pltpu.VMEM((hidden_size, width), bf16),
            pltpu.VMEM((store_rows, hidden_size), bf16),
            pltpu.SemaphoreType.DMA((7 + PLANE,)),
        ],
        flops=4 * store_rows * width * hidden_size,
        grant=MLP_GRANT,
        first_out=HBM_SPEC,
    )
    item_out, item_parts = mlp[0], mlp[1:]
    item_plane = [item_parts[0]] + [in_plane(item_parts[step], step) for step in steps]

    user = call(
        functools.partial(attend_kernel, hist_rows, shifts),
        jax.ShapeDtypeStruct((rows, part), bf16),
        query_plane + kv_blocks,
        flops=4 * rows * rows * (shifts + 1) * part,
    )
    users = [user]
    for step in range(1, planes):
        bit = step & -step
        users.append(swap(users[step - bit], bit))
    together = min(planes, LANES // cand_slots, 4)
    results = []
    for first in range(0, planes, together):
        place = call(
            functools.partial(place_kernel, hist_rows, store_rows),
            jax.ShapeDtypeStruct((rows, LANES), jnp.int32),
            metas[first : first + together],
        )
        total = []
        for at in sorted(range(together), key=lambda at: (at == 3, at == 1)):
            total = [
                call(
                    functools.partial(score_kernel, hist_rows, cand_slots, at, not total),
                    jax.ShapeDtypeStruct((rows, LANES), jnp.float32),
                    [users[first + at]] + item_plane + [place] + total,
                    [pltpu.VMEM((rows, PLANE * store_rows), jnp.float32)],
                    flops=2 * rows * part * PLANE * store_rows,
                )
            ]
        results.append(
            call(
                functools.partial(send_kernel, hist_rows, cand_slots, planes == together),
                jax.ShapeDtypeStruct(
                    (together * PLANE, cand_slots // 2, 2 * hist_rows), jnp.float32
                ),
                total,
            )
        )
    if len(results) == 1:
        partial = results[0]
    else:
        order = plane ^ jnp.arange(planes, dtype=jnp.int32)
        partial = jnp.concatenate(results).reshape(planes, PLANE, cand_slots // 2, 2 * hist_rows)
        partial = partial[order].reshape(block_count, cand_slots // 2, 2 * hist_rows)
    gathered = lax.all_to_all(partial, "blk", split_axis=0, concat_axis=0, tiled=True)
    scores = call(
        finish_kernel,
        jax.ShapeDtypeStruct((cand_slots, hist_rows), jnp.float32),
        [gathered, cand_count.reshape(1, -1)],
    )
    return (item_out, scores.T)


def solution(mesh):
    in_specs = (
        P(("groups", "blk"), None),
        P("groups"),
        P(),
        P(),
        P(("groups", "blk"), None),
        P(),
        P(("groups", "blk"), None, None),
        P(("groups", "blk")),
        P(("groups", "blk"), None),
        P(("groups", "blk")),
    )
    out_specs = (P(("groups", "blk"), None), P(("groups", "blk"), None))
    return jax.shard_map(
        per_device, mesh=mesh, in_specs=in_specs, out_specs=out_specs, check_vma=False
    )
```

```python
import functools

import jax
import jax.numpy as jnp
from jax import lax
from jax.experimental import pallas as pl
from jax.experimental.pallas import tpu as pltpu
from jax.sharding import PartitionSpec as P


HEADS = 8
WIN = 512
PLANE = 4
LANES = 128
TILE = 512

VMEM_SPEC = pl.BlockSpec(memory_space=pltpu.VMEM)
HBM_SPEC = pl.BlockSpec(memory_space=pltpu.MemorySpace.HBM)
VMEM_LIMIT = 24 * 1024 * 1024
COVER = 6_000_000_000


def call(body, out_shape, args, scratch=(), flops=0, first_out=None):
    size = sum(a.size * a.dtype.itemsize for a in args)
    out_specs = jax.tree.map(lambda _: VMEM_SPEC, out_shape)
    if first_out is not None:
        out_specs[0] = first_out
    return pl.pallas_call(
        body,
        out_shape=out_shape,
        in_specs=[VMEM_SPEC] * len(args),
        out_specs=out_specs,
        scratch_shapes=list(scratch),
        compiler_params=pltpu.CompilerParams(vmem_limit_bytes=VMEM_LIMIT),
        cost_estimate=pl.CostEstimate(flops=flops, bytes_accessed=size, transcendentals=0),
    )(*args)


def in_plane(value, step):
    count = lax.axis_size("blk")
    pairs = [(s, (s // PLANE) * PLANE + ((s % PLANE) ^ step)) for s in range(count)]
    return lax.ppermute(value, "blk", pairs)


def forward(value, step):
    count = lax.axis_size("blk")
    return lax.ppermute(value, "blk", [(s, (s + step * PLANE) % count) for s in range(count)])


def swap(value, step):
    count = lax.axis_size("blk")
    return lax.ppermute(value, "blk", [(s, s ^ (step * PLANE)) for s in range(count)])


def my_place():
    index = lax.axis_index("blk")
    return index // PLANE, index % PLANE


def part_windows(part):
    column = my_place()[1]
    return [pl.ds(pl.multiple_of((column ^ step) * part, part), part) for step in range(PLANE)]


def copies_of(pairs, sems):
    return [
        pltpu.make_async_copy(source, target, sems.at[at])
        for at, (source, target) in enumerate(pairs)
    ]


def kv_pieces_kernel(kv_ref, *rest):
    outs, (key_buf, value_buf) = rest[:PLANE], rest[PLANE:]
    part = outs[0].shape[1] // 2
    windows = part_windows(part)
    key_buf[...] = kv_ref[:, 0, :]
    value_buf[...] = kv_ref[:, 1, :]
    for step in range(PLANE):
        outs[step][:, :part] = key_buf[:, windows[step]]
        outs[step][:, part:] = value_buf[:, windows[step]]


def query_kernel(event_ref, weight_ref, cand_ref, table_ref, start_ref, *rest):
    query_outs, query_buf = rest[:PLANE], rest[PLANE]
    index = lax.axis_index("blk")
    hist_rows = event_ref.shape[0]
    windows = part_windows(query_outs[0].shape[1])
    ids = cand_ref[...]
    ids = jnp.concatenate([ids, ids], axis=1)
    table_row = ids // LANES
    table_lane = ids % LANES

    def look(row, found):
        values = jnp.broadcast_to(table_ref[pl.ds(row, 1), :], ids.shape)
        picked = jnp.take_along_axis(values, table_lane, axis=1, mode="promise_in_bounds")
        return jnp.where(table_row == row, picked, found)

    slot = lax.fori_loop(0, table_ref.shape[0], look, jnp.zeros_like(ids), unroll=8)
    first_half = lax.broadcasted_iota(jnp.int32, ids.shape, 1) < hist_rows
    slot_meta = jnp.where(first_half, slot // 256, slot % 256)
    starts = start_ref[...]
    starts = jnp.concatenate([starts, starts], axis=1)
    place = index * hist_rows + lax.broadcasted_iota(jnp.int32, starts.shape, 1) % hist_rows
    reach = index * hist_rows + hist_rows - WIN
    offset = place - jnp.maximum(starts, reach)
    offset = jnp.broadcast_to(offset, ids.shape)
    offset_meta = jnp.where(first_half, offset // 16, offset % 16)
    meta = jnp.concatenate([slot_meta, offset_meta], axis=1)
    meta = meta.astype(jnp.float32).astype(jnp.bfloat16)
    query = jnp.dot(event_ref[...], weight_ref[...], preferred_element_type=jnp.float32)
    query_buf[...] = query.astype(jnp.bfloat16)
    for step in range(PLANE):
        query_outs[step][:hist_rows, :] = query_buf[:, windows[step]]
        query_outs[step][hist_rows:, :] = meta


def join_kernel(*refs):
    pieces, (rest_ref, late_ref) = refs[:PLANE], refs[PLANE:]
    column = my_place()[1]
    rows = pieces[0].shape[0]
    for step in range(1, PLANE):
        rest_ref[(step - 1) * rows : step * rows, :] = pieces[step][...]
    for block in range(1, PLANE):
        for step in range(PLANE):

            @pl.when((column ^ block) == step)
            def _(block=block, step=step):
                late_ref[(block - 1) * rows : block * rows, :] = pieces[step][...]


def key_positions(hist_rows, count, shift):
    plane, column = my_place()
    at = lax.broadcasted_iota(jnp.int32, (1, count), 1)
    block = at // hist_rows
    block = (column ^ block) if count == PLANE * hist_rows else 1 + block
    return ((plane - shift) * PLANE + block) * hist_rows + at % hist_rows


def query_positions(hist_rows):
    plane, column = my_place()
    at = lax.broadcasted_iota(jnp.int32, (PLANE * hist_rows, 1), 0)
    return (plane * PLANE + (column ^ (at // hist_rows))) * hist_rows + at % hist_rows


def add_attention(total_ref, query, query_pos, offset, keys, key_pos):
    part = query.shape[1]
    head_size = part * PLANE // HEADS
    inside = (key_pos <= query_pos) & (key_pos >= query_pos - offset)
    for head in range(part // head_size):
        window = slice(head * head_size, (head + 1) * head_size)
        logits = head_size**-0.5 * lax.dot_general(
            query[:, window],
            keys[:, window],
            (((1,), (1,)), ((), ())),
            preferred_element_type=jnp.float32,
        )
        weights = jnp.where(inside, jax.nn.silu(logits) * (1.0 / WIN), 0.0)
        total_ref[:, window] += jnp.dot(
            weights.astype(jnp.bfloat16),
            keys[:, part + head * head_size : part + (head + 1) * head_size],
            preferred_element_type=jnp.float32,
        )


def near_kernel(hist_rows, *refs):
    queries, blocks = refs[:PLANE], refs[PLANE:-4]
    total_ref, query_ref, offset_ref, meta_ref = refs[-4:]
    slots = queries[0].shape[0] - hist_rows
    part = queries[0].shape[1]
    for step in range(PLANE):
        rows = slice(step * hist_rows, (step + 1) * hist_rows)
        query_ref[rows, :] = queries[step][:hist_rows, :]
        meta = queries[step][hist_rows:, LANES:].astype(jnp.float32)
        offset = meta[:, :hist_rows] * 16 + meta[:, hist_rows:]
        offset = jnp.transpose(offset)[:, :1].astype(jnp.int32)
        offset_ref[rows, :] = jnp.broadcast_to(offset, (hist_rows, LANES))
        row, lane = divmod(step * LANES, part)
        meta_ref[row * slots : (row + 1) * slots, lane : lane + LANES] = queries[step][
            hist_rows:, :LANES
        ]
    total_ref[...] = jnp.zeros_like(total_ref)
    query_pos = query_positions(hist_rows)
    blocks = [block[...] for block in blocks]
    planes = [jnp.concatenate(blocks[:PLANE], axis=0)]
    planes += [jnp.concatenate(blocks[at : at + 2], axis=0) for at in range(PLANE, len(blocks), 2)]
    for shift, keys in enumerate(planes):
        key_pos = key_positions(hist_rows, keys.shape[0], shift)
        add_attention(total_ref, query_ref[...], query_pos, offset_ref[:, :1], keys, key_pos)


def far_kernel(
    hist_rows, shift, key_ref, before_ref, query_ref, offset_ref, meta_ref, out_ref, total_ref
):
    rows = total_ref.shape[0]
    total_ref[...] = before_ref[...]
    key_pos = key_positions(hist_rows, key_ref.shape[0], shift)
    add_attention(
        total_ref,
        query_ref[...],
        query_positions(hist_rows),
        offset_ref[:, :1],
        key_ref[...],
        key_pos,
    )
    out_ref[:rows, :] = total_ref[...].astype(jnp.bfloat16)
    out_ref[rows:, :] = meta_ref[...]


def mlp_kernel(row_ref, up_ref, down_ref, out_hbm, *rest):
    parts, (hidden_ref, sems) = rest[:PLANE], rest[PLANE:]
    windows = part_windows(parts[0].shape[1])
    saves = copies_of(
        [(parts[step], out_hbm.at[:, windows[step]]) for step in range(PLANE)], sems
    )
    for at in range(0, up_ref.shape[1], TILE):
        hidden = jnp.dot(
            row_ref[...], up_ref[:, at : at + TILE], preferred_element_type=jnp.float32
        )
        hidden_ref[:, at : at + TILE] = jax.nn.silu(hidden).astype(jnp.bfloat16)
    for step in range(PLANE):
        mixed = jnp.dot(
            hidden_ref[...], down_ref[:, windows[step]], preferred_element_type=jnp.float32
        )
        mixed = row_ref[:, windows[step]].astype(jnp.float32) + mixed
        parts[step][...] = mixed.astype(jnp.bfloat16)
        saves[step].start()
    for copy in saves:
        copy.wait()


def item_places(hist_rows, slots, store_rows, at, user_ref):
    plane, column = my_place()
    rows, part = PLANE * hist_rows, user_ref.shape[1]
    pieces = []
    for step in range(PLANE):
        row, lane = divmod(step * LANES, part)
        row = rows + row * slots
        meta = user_ref[row : row + slots, lane : lane + LANES].astype(jnp.float32)
        pieces.append(meta[:, :hist_rows] * 256 + meta[:, hist_rows:])
    ids = [jnp.concatenate(pieces, axis=1)]
    low, high = at * slots, LANES - (at + 1) * slots
    if low:
        ids.insert(0, jnp.zeros((low, rows), jnp.float32))
    if high:
        ids.append(jnp.zeros((high, rows), jnp.float32))
    local = jnp.transpose(jnp.concatenate(ids, axis=0)).astype(jnp.int32)
    local = local - plane * (PLANE * store_rows)
    owned = (local >= 0) & (local < PLANE * store_rows)
    owned &= lax.broadcasted_iota(jnp.int32, local.shape, 1) // slots == at
    place = ((local // store_rows) ^ column) * store_rows + local % store_rows
    return jnp.where(owned, place, -1)


def score_kernel(hist_rows, slots, at, first, *refs):
    user_ref, items = refs[0], refs[1 : 1 + PLANE]
    before_ref = None if first else refs[1 + PLANE]
    out_ref, dense_ref = refs[-2:]
    store_rows = items[0].shape[0]
    for step in range(PLANE):
        dense_ref[:, step * store_rows : (step + 1) * store_rows] = lax.dot_general(
            user_ref[: PLANE * hist_rows, :],
            items[step][...],
            (((1,), (1,)), ((), ())),
            preferred_element_type=jnp.float32,
        )
    places = item_places(hist_rows, slots, store_rows, at, user_ref)
    for tile in range(PLANE):
        rows = slice(tile * hist_rows, (tile + 1) * hist_rows)
        place = places[rows, :]
        lane_at = place & (LANES - 1)
        mine = place >> 7
        total = jnp.zeros(place.shape, jnp.float32) if first else before_ref[rows, :]
        for chunk in range(PLANE * store_rows // LANES):
            picked = jnp.take_along_axis(
                dense_ref[rows, chunk * LANES : (chunk + 1) * LANES],
                lane_at,
                axis=1,
                mode="promise_in_bounds",
            )
            total = jnp.where(mine == chunk, picked, total)
        out_ref[rows, :] = total


def send_kernel(hist_rows, slots, ordered, total_ref, out_ref):
    plane, column = my_place()
    turned = jnp.transpose(total_ref[...])
    half = slots // 2
    for at in range(out_ref.shape[0] // PLANE):
        for step in range(PLANE):
            lanes = slice(step * hist_rows, (step + 1) * hist_rows)
            block = jnp.concatenate(
                [
                    turned[at * slots : at * slots + half, lanes],
                    turned[at * slots + half : (at + 1) * slots, lanes],
                ],
                axis=1,
            )
            to_plane = plane ^ at if ordered else at
            out_ref[to_plane * PLANE + (column ^ step)] = block


def finish_kernel(part_ref, count_ref, out_ref):
    total = part_ref[0]
    for at in range(1, part_ref.shape[0]):
        total = total + part_ref[at]
    hist_rows = out_ref.shape[1]
    total = jnp.concatenate([total[:, :hist_rows], total[:, hist_rows:]], axis=0)
    live = lax.broadcasted_iota(jnp.int32, total.shape, 0) < count_ref[...]
    out_ref[...] = jnp.where(live, total, 0.0)


def per_device(
    item_rows, item_slot, w_up, w_down, events, w_query, history_kv, window_start, cand, cand_count
):
    block_count = lax.axis_size("blk")
    planes = block_count // PLANE
    plane, _ = my_place()
    hist_rows = events.shape[0]
    store_rows, width = item_rows.shape
    hidden_size = w_up.shape[1]
    cand_slots = cand.shape[1]
    att = history_kv.shape[2]
    part = att // PLANE
    rows = PLANE * hist_rows
    bf16 = jnp.bfloat16
    reach = WIN // hist_rows - 1
    shifts = -(-reach // PLANE)
    steps = range(1, PLANE)

    kv_own = call(
        kv_pieces_kernel,
        [jax.ShapeDtypeStruct((hist_rows, 2 * part), bf16)] * PLANE,
        [history_kv],
        [pltpu.VMEM((hist_rows, att), bf16)] * 2,
        flops=COVER,
    )
    kv_plane = [kv_own[0]] + [in_plane(kv_own[step], step) for step in steps]
    query_own = call(
        query_kernel,
        [jax.ShapeDtypeStruct((hist_rows + cand_slots, part), bf16)] * PLANE,
        [events, w_query, cand.T, item_slot.reshape(-1, LANES), window_start.reshape(1, -1)],
        [pltpu.VMEM((hist_rows, att), bf16)],
        flops=COVER,
    )
    query_plane = [query_own[0]] + [in_plane(query_own[step], step) for step in steps]
    kv_rest, kv_late = call(
        join_kernel, [jax.ShapeDtypeStruct((rows - hist_rows, 2 * part), bf16)] * 2, kv_plane
    )
    kv_near = list(kv_plane)
    for shift in range(1, shifts):
        kv_near += [forward(kv_plane[0], shift), forward(kv_rest, shift)]
    kv_far = forward(kv_late, shifts)

    mlp = call(
        mlp_kernel,
        [jax.ShapeDtypeStruct((store_rows, width), bf16)]
        + [jax.ShapeDtypeStruct((store_rows, part), bf16)] * PLANE,
        [item_rows, w_up, w_down],
        [
            pltpu.VMEM((store_rows, hidden_size), bf16),
            pltpu.SemaphoreType.DMA((PLANE,)),
        ],
        flops=4 * store_rows * width * hidden_size,
        first_out=HBM_SPEC,
    )
    item_out, item_parts = mlp[0], mlp[1:]
    item_plane = [item_parts[0]] + [in_plane(item_parts[step], step) for step in steps]

    near = call(
        functools.partial(near_kernel, hist_rows),
        [
            jax.ShapeDtypeStruct((rows, part), jnp.float32),
            jax.ShapeDtypeStruct((rows, part), bf16),
            jax.ShapeDtypeStruct((rows, LANES), jnp.int32),
            jax.ShapeDtypeStruct((PLANE * cand_slots * LANES // part, part), bf16),
        ],
        query_plane + kv_near,
        flops=4 * rows * rows * shifts * part,
    )
    user = call(
        functools.partial(far_kernel, hist_rows, shifts),
        jax.ShapeDtypeStruct((rows + near[3].shape[0], part), bf16),
        [kv_far, *near],
        [pltpu.VMEM((rows, part), jnp.float32)],
        flops=4 * rows * rows * part,
    )
    users = [user]
    for step in range(1, planes):
        bit = step & -step
        users.append(swap(users[step - bit], bit))
    together = min(planes, LANES // cand_slots, 4)
    results = []
    for first in range(0, planes, together):
        total = []
        for at in sorted(range(together), key=lambda at: (at == 3, at == 1)):
            total = [
                call(
                    functools.partial(score_kernel, hist_rows, cand_slots, at, not total),
                    jax.ShapeDtypeStruct((rows, LANES), jnp.float32),
                    [users[first + at]] + item_plane + total,
                    [pltpu.VMEM((rows, PLANE * store_rows), jnp.float32)],
                    flops=2 * rows * part * PLANE * store_rows,
                )
            ]
        results.append(
            call(
                functools.partial(send_kernel, hist_rows, cand_slots, planes == together),
                jax.ShapeDtypeStruct(
                    (together * PLANE, cand_slots // 2, 2 * hist_rows), jnp.float32
                ),
                total,
            )
        )
    if len(results) == 1:
        partial = results[0]
    else:
        order = plane ^ jnp.arange(planes, dtype=jnp.int32)
        partial = jnp.concatenate(results).reshape(planes, PLANE, cand_slots // 2, 2 * hist_rows)
        partial = partial[order].reshape(block_count, cand_slots // 2, 2 * hist_rows)
    gathered = lax.all_to_all(partial, "blk", split_axis=0, concat_axis=0, tiled=True)
    scores = call(
        finish_kernel,
        jax.ShapeDtypeStruct((cand_slots, hist_rows), jnp.float32),
        [gathered, cand_count.reshape(1, -1)],
    )
    return (item_out, scores.T)


def solution(mesh):
    in_specs = (
        P(("groups", "blk"), None),
        P("groups"),
        P(),
        P(),
        P(("groups", "blk"), None),
        P(),
        P(("groups", "blk"), None, None),
        P(("groups", "blk")),
        P(("groups", "blk"), None),
        P(("groups", "blk")),
    )
    out_specs = (P(("groups", "blk"), None), P(("groups", "blk"), None))
    return jax.shard_map(
        per_device, mesh=mesh, in_specs=in_specs, out_specs=out_specs, check_vma=False
    )
```

```python
import functools

import jax
import jax.numpy as jnp
from jax import lax
from jax.experimental import pallas as pl
from jax.experimental.pallas import tpu as pltpu
from jax.sharding import PartitionSpec as P


HEADS = 8
WIN = 512
PLANE = 4
LANES = 128
TILE = 512

VMEM_SPEC = pl.BlockSpec(memory_space=pltpu.VMEM)
HBM_SPEC = pl.BlockSpec(memory_space=pltpu.MemorySpace.HBM)
VMEM_LIMIT = 24 * 1024 * 1024
COVER = 6_000_000_000


def call(body, out_shape, args, scratch=(), flops=0, first_out=None):
    size = sum(a.size * a.dtype.itemsize for a in args)
    out_specs = jax.tree.map(lambda _: VMEM_SPEC, out_shape)
    if first_out is not None:
        out_specs[0] = first_out
    return pl.pallas_call(
        body,
        out_shape=out_shape,
        in_specs=[VMEM_SPEC] * len(args),
        out_specs=out_specs,
        scratch_shapes=list(scratch),
        compiler_params=pltpu.CompilerParams(vmem_limit_bytes=VMEM_LIMIT),
        cost_estimate=pl.CostEstimate(flops=flops, bytes_accessed=size, transcendentals=0),
    )(*args)


def in_plane(value, step):
    count = lax.axis_size("blk")
    pairs = [(s, (s // PLANE) * PLANE + ((s % PLANE) ^ step)) for s in range(count)]
    return lax.ppermute(value, "blk", pairs)


def forward(value, step):
    count = lax.axis_size("blk")
    return lax.ppermute(value, "blk", [(s, (s + step * PLANE) % count) for s in range(count)])


def swap(value, step):
    count = lax.axis_size("blk")
    return lax.ppermute(value, "blk", [(s, s ^ (step * PLANE)) for s in range(count)])


def my_place():
    index = lax.axis_index("blk")
    return index // PLANE, index % PLANE


def part_windows(part):
    column = my_place()[1]
    return [pl.ds(pl.multiple_of((column ^ step) * part, part), part) for step in range(PLANE)]


def copies_of(pairs, sems):
    return [
        pltpu.make_async_copy(source, target, sems.at[at])
        for at, (source, target) in enumerate(pairs)
    ]


def kv_pieces_kernel(kv_ref, *rest):
    outs, (key_buf, value_buf) = rest[:PLANE], rest[PLANE:]
    part = outs[0].shape[1] // 2
    windows = part_windows(part)
    key_buf[...] = kv_ref[:, 0, :]
    value_buf[...] = kv_ref[:, 1, :]
    for step in range(PLANE):
        outs[step][:, :part] = key_buf[:, windows[step]]
        outs[step][:, part:] = value_buf[:, windows[step]]


def query_kernel(event_ref, weight_ref, cand_ref, table_ref, start_ref, *rest):
    query_outs, query_buf = rest[:PLANE], rest[PLANE]
    index = lax.axis_index("blk")
    hist_rows = event_ref.shape[0]
    windows = part_windows(query_outs[0].shape[1])
    ids = cand_ref[...]
    ids = jnp.concatenate([ids, ids], axis=1)
    table_row = ids // LANES
    table_lane = ids % LANES

    def look(row, found):
        values = jnp.broadcast_to(table_ref[pl.ds(row, 1), :], ids.shape)
        picked = jnp.take_along_axis(values, table_lane, axis=1, mode="promise_in_bounds")
        return jnp.where(table_row == row, picked, found)

    slot = lax.fori_loop(0, table_ref.shape[0], look, jnp.zeros_like(ids), unroll=8)
    first_half = lax.broadcasted_iota(jnp.int32, ids.shape, 1) < hist_rows
    slot_meta = jnp.where(first_half, slot // 256, slot % 256)
    starts = start_ref[...]
    starts = jnp.concatenate([starts, starts], axis=1)
    place = index * hist_rows + lax.broadcasted_iota(jnp.int32, starts.shape, 1) % hist_rows
    reach = index * hist_rows + hist_rows - WIN
    offset = place - jnp.maximum(starts, reach)
    offset = jnp.broadcast_to(offset, ids.shape)
    offset_meta = jnp.where(first_half, offset // 16, offset % 16)
    meta = jnp.concatenate([slot_meta, offset_meta], axis=1)
    meta = meta.astype(jnp.float32).astype(jnp.bfloat16)
    query = jnp.dot(event_ref[...], weight_ref[...], preferred_element_type=jnp.float32)
    query_buf[...] = query.astype(jnp.bfloat16)
    for step in range(PLANE):
        query_outs[step][:hist_rows, :] = query_buf[:, windows[step]]
        query_outs[step][hist_rows:, :] = meta


def late_blocks(column):
    early = jnp.maximum(column, 1)
    return early, jnp.where(early == 1, 2, 1), jnp.where(early == PLANE - 1, 2, PLANE - 1)


def early_kernel(own_ref, near_ref, out_ref):
    column = my_place()[1]

    @pl.when(column == 0)
    def _():
        out_ref[...] = near_ref[...]

    @pl.when(column > 0)
    def _():
        out_ref[...] = own_ref[...]


def join_kernel(*refs):
    pieces, (rest_ref, late_ref) = refs[:PLANE], refs[PLANE:]
    column = my_place()[1]
    rows = pieces[0].shape[0]
    for step in range(1, PLANE):
        rest_ref[(step - 1) * rows : step * rows, :] = pieces[step][...]
    for at, block in enumerate(late_blocks(column)[1:]):
        for step in range(1, PLANE):

            @pl.when((column ^ block) == step)
            def _(at=at, step=step):
                late_ref[at * rows : (at + 1) * rows, :] = pieces[step][...]


def key_positions(hist_rows, count, shift):
    plane, column = my_place()
    at = lax.broadcasted_iota(jnp.int32, (1, count), 1)
    block = at // hist_rows
    if count == PLANE * hist_rows:
        block = column ^ block
    else:
        first, second, third = late_blocks(column)
        block = jnp.where(block == 0, first, jnp.where(block == 1, second, third))
    return ((plane - shift) * PLANE + block) * hist_rows + at % hist_rows


def query_positions(hist_rows):
    plane, column = my_place()
    at = lax.broadcasted_iota(jnp.int32, (PLANE * hist_rows, 1), 0)
    return (plane * PLANE + (column ^ (at // hist_rows))) * hist_rows + at % hist_rows


def add_attention(total_ref, query, query_pos, offset, keys, key_pos):
    part = query.shape[1]
    head_size = part * PLANE // HEADS
    inside = (key_pos <= query_pos) & (key_pos >= query_pos - offset)
    for head in range(part // head_size):
        window = slice(head * head_size, (head + 1) * head_size)
        logits = head_size**-0.5 * lax.dot_general(
            query[:, window],
            keys[:, window],
            (((1,), (1,)), ((), ())),
            preferred_element_type=jnp.float32,
        )
        weights = jnp.where(inside, jax.nn.silu(logits) * (1.0 / WIN), 0.0)
        total_ref[:, window] += jnp.dot(
            weights.astype(jnp.bfloat16),
            keys[:, part + head * head_size : part + (head + 1) * head_size],
            preferred_element_type=jnp.float32,
        )


def near_kernel(hist_rows, *refs):
    queries, blocks = refs[:PLANE], refs[PLANE:-4]
    total_ref, query_ref, offset_ref, meta_ref = refs[-4:]
    slots = queries[0].shape[0] - hist_rows
    part = queries[0].shape[1]
    for step in range(PLANE):
        rows = slice(step * hist_rows, (step + 1) * hist_rows)
        query_ref[rows, :] = queries[step][:hist_rows, :]
        meta = queries[step][hist_rows:, LANES:].astype(jnp.float32)
        offset = meta[:, :hist_rows] * 16 + meta[:, hist_rows:]
        offset = jnp.transpose(offset)[:, :1].astype(jnp.int32)
        offset_ref[rows, :] = jnp.broadcast_to(offset, (hist_rows, LANES))
        row, lane = divmod(step * LANES, part)
        meta_ref[row * slots : (row + 1) * slots, lane : lane + LANES] = queries[step][
            hist_rows:, :LANES
        ]
    total_ref[...] = jnp.zeros_like(total_ref)
    query_pos = query_positions(hist_rows)
    blocks = [block[...] for block in blocks]
    planes = [jnp.concatenate(blocks[:PLANE], axis=0)]
    planes += [jnp.concatenate(blocks[at : at + 2], axis=0) for at in range(PLANE, len(blocks), 2)]
    for shift, keys in enumerate(planes):
        key_pos = key_positions(hist_rows, keys.shape[0], shift)
        add_attention(total_ref, query_ref[...], query_pos, offset_ref[:, :1], keys, key_pos)


def far_kernel(
    hist_rows,
    shift,
    early_ref,
    late_ref,
    before_ref,
    query_ref,
    offset_ref,
    meta_ref,
    out_ref,
    total_ref,
):
    rows = total_ref.shape[0]
    total_ref[...] = before_ref[...]
    keys = jnp.concatenate([early_ref[...], late_ref[...]], axis=0)
    key_pos = key_positions(hist_rows, keys.shape[0], shift)
    query_pos = query_positions(hist_rows)
    add_attention(total_ref, query_ref[...], query_pos, offset_ref[:, :1], keys, key_pos)
    out_ref[:rows, :] = total_ref[...].astype(jnp.bfloat16)
    out_ref[rows:, :] = meta_ref[...]


def mlp_kernel(row_ref, up_ref, down_ref, out_hbm, *rest):
    parts, (hidden_ref, sems) = rest[:PLANE], rest[PLANE:]
    windows = part_windows(parts[0].shape[1])
    saves = copies_of(
        [(parts[step], out_hbm.at[:, windows[step]]) for step in range(PLANE)], sems
    )
    for at in range(0, up_ref.shape[1], TILE):
        hidden = jnp.dot(
            row_ref[...], up_ref[:, at : at + TILE], preferred_element_type=jnp.float32
        )
        hidden_ref[:, at : at + TILE] = jax.nn.silu(hidden).astype(jnp.bfloat16)
    for step in range(PLANE):
        mixed = jnp.dot(
            hidden_ref[...], down_ref[:, windows[step]], preferred_element_type=jnp.float32
        )
        mixed = row_ref[:, windows[step]].astype(jnp.float32) + mixed
        parts[step][...] = mixed.astype(jnp.bfloat16)
        saves[step].start()
    for copy in saves:
        copy.wait()


def item_places(hist_rows, slots, store_rows, at, user_ref):
    plane, column = my_place()
    rows, part = PLANE * hist_rows, user_ref.shape[1]
    pieces = []
    for step in range(PLANE):
        row, lane = divmod(step * LANES, part)
        row = rows + row * slots
        meta = user_ref[row : row + slots, lane : lane + LANES].astype(jnp.float32)
        pieces.append(meta[:, :hist_rows] * 256 + meta[:, hist_rows:])
    ids = [jnp.concatenate(pieces, axis=1)]
    low, high = at * slots, LANES - (at + 1) * slots
    if low:
        ids.insert(0, jnp.zeros((low, rows), jnp.float32))
    if high:
        ids.append(jnp.zeros((high, rows), jnp.float32))
    local = jnp.transpose(jnp.concatenate(ids, axis=0)).astype(jnp.int32)
    local = local - plane * (PLANE * store_rows)
    owned = (local >= 0) & (local < PLANE * store_rows)
    owned &= lax.broadcasted_iota(jnp.int32, local.shape, 1) // slots == at
    place = ((local // store_rows) ^ column) * store_rows + local % store_rows
    return jnp.where(owned, place, -1)


def score_kernel(hist_rows, slots, at, first, *refs):
    user_ref, items = refs[0], refs[1 : 1 + PLANE]
    before_ref = None if first else refs[1 + PLANE]
    out_ref, dense_ref = refs[-2:]
    store_rows = items[0].shape[0]
    for step in range(PLANE):
        dense_ref[:, step * store_rows : (step + 1) * store_rows] = lax.dot_general(
            user_ref[: PLANE * hist_rows, :],
            items[step][...],
            (((1,), (1,)), ((), ())),
            preferred_element_type=jnp.float32,
        )
    places = item_places(hist_rows, slots, store_rows, at, user_ref)
    for tile in range(PLANE):
        rows = slice(tile * hist_rows, (tile + 1) * hist_rows)
        place = places[rows, :]
        lane_at = place & (LANES - 1)
        mine = place >> 7
        total = jnp.zeros(place.shape, jnp.float32) if first else before_ref[rows, :]
        for chunk in range(PLANE * store_rows // LANES):
            picked = jnp.take_along_axis(
                dense_ref[rows, chunk * LANES : (chunk + 1) * LANES],
                lane_at,
                axis=1,
                mode="promise_in_bounds",
            )
            total = jnp.where(mine == chunk, picked, total)
        out_ref[rows, :] = total


def send_kernel(hist_rows, slots, ordered, total_ref, out_ref):
    plane, column = my_place()
    turned = jnp.transpose(total_ref[...])
    half = slots // 2
    for at in range(out_ref.shape[0] // PLANE):
        for step in range(PLANE):
            lanes = slice(step * hist_rows, (step + 1) * hist_rows)
            block = jnp.concatenate(
                [
                    turned[at * slots : at * slots + half, lanes],
                    turned[at * slots + half : (at + 1) * slots, lanes],
                ],
                axis=1,
            )
            to_plane = plane ^ at if ordered else at
            out_ref[to_plane * PLANE + (column ^ step)] = block


def finish_kernel(part_ref, count_ref, out_ref):
    total = part_ref[0]
    for at in range(1, part_ref.shape[0]):
        total = total + part_ref[at]
    hist_rows = out_ref.shape[1]
    total = jnp.concatenate([total[:, :hist_rows], total[:, hist_rows:]], axis=0)
    live = lax.broadcasted_iota(jnp.int32, total.shape, 0) < count_ref[...]
    out_ref[...] = jnp.where(live, total, 0.0)


def per_device(
    item_rows, item_slot, w_up, w_down, events, w_query, history_kv, window_start, cand, cand_count
):
    block_count = lax.axis_size("blk")
    planes = block_count // PLANE
    plane, _ = my_place()
    hist_rows = events.shape[0]
    store_rows, width = item_rows.shape
    hidden_size = w_up.shape[1]
    cand_slots = cand.shape[1]
    att = history_kv.shape[2]
    part = att // PLANE
    rows = PLANE * hist_rows
    bf16 = jnp.bfloat16
    reach = WIN // hist_rows - 1
    shifts = -(-reach // PLANE)
    steps = range(1, PLANE)

    kv_own = call(
        kv_pieces_kernel,
        [jax.ShapeDtypeStruct((hist_rows, 2 * part), bf16)] * PLANE,
        [history_kv],
        [pltpu.VMEM((hist_rows, att), bf16)] * 2,
        flops=COVER,
    )
    kv_plane = [kv_own[0]] + [in_plane(kv_own[step], step) for step in steps]
    query_own = call(
        query_kernel,
        [jax.ShapeDtypeStruct((hist_rows + cand_slots, part), bf16)] * PLANE,
        [events, w_query, cand.T, item_slot.reshape(-1, LANES), window_start.reshape(1, -1)],
        [pltpu.VMEM((hist_rows, att), bf16)],
        flops=COVER,
    )
    query_plane = [query_own[0]] + [in_plane(query_own[step], step) for step in steps]
    kv_early = call(early_kernel, jax.ShapeDtypeStruct((hist_rows, 2 * part), bf16), kv_plane[:2])
    kv_rest, kv_late = call(
        join_kernel,
        [
            jax.ShapeDtypeStruct((rows - hist_rows, 2 * part), bf16),
            jax.ShapeDtypeStruct((rows - 2 * hist_rows, 2 * part), bf16),
        ],
        kv_plane,
    )
    kv_near = list(kv_plane)
    for shift in range(1, shifts):
        kv_near += [forward(kv_plane[0], shift), forward(kv_rest, shift)]
    kv_far = [forward(kv_early, shifts), forward(kv_late, shifts)]

    mlp = call(
        mlp_kernel,
        [jax.ShapeDtypeStruct((store_rows, width), bf16)]
        + [jax.ShapeDtypeStruct((store_rows, part), bf16)] * PLANE,
        [item_rows, w_up, w_down],
        [
            pltpu.VMEM((store_rows, hidden_size), bf16),
            pltpu.SemaphoreType.DMA((PLANE,)),
        ],
        flops=4 * store_rows * width * hidden_size,
        first_out=HBM_SPEC,
    )
    item_out, item_parts = mlp[0], mlp[1:]
    item_plane = [item_parts[0]] + [in_plane(item_parts[step], step) for step in steps]

    near = call(
        functools.partial(near_kernel, hist_rows),
        [
            jax.ShapeDtypeStruct((rows, part), jnp.float32),
            jax.ShapeDtypeStruct((rows, part), bf16),
            jax.ShapeDtypeStruct((rows, LANES), jnp.int32),
            jax.ShapeDtypeStruct((PLANE * cand_slots * LANES // part, part), bf16),
        ],
        query_plane + kv_near,
        flops=4 * rows * rows * shifts * part,
    )
    user = call(
        functools.partial(far_kernel, hist_rows, shifts),
        jax.ShapeDtypeStruct((rows + near[3].shape[0], part), bf16),
        [*kv_far, *near],
        [pltpu.VMEM((rows, part), jnp.float32)],
        flops=4 * rows * rows * part,
    )
    users = [user]
    for step in range(1, planes):
        bit = step & -step
        users.append(swap(users[step - bit], bit))
    together = min(planes, LANES // cand_slots, 4)
    results = []
    for first in range(0, planes, together):
        total = []
        for at in sorted(range(together), key=lambda at: (at == 3, at == 1)):
            total = [
                call(
                    functools.partial(score_kernel, hist_rows, cand_slots, at, not total),
                    jax.ShapeDtypeStruct((rows, LANES), jnp.float32),
                    [users[first + at]] + item_plane + total,
                    [pltpu.VMEM((rows, PLANE * store_rows), jnp.float32)],
                    flops=2 * rows * part * PLANE * store_rows,
                )
            ]
        results.append(
            call(
                functools.partial(send_kernel, hist_rows, cand_slots, planes == together),
                jax.ShapeDtypeStruct(
                    (together * PLANE, cand_slots // 2, 2 * hist_rows), jnp.float32
                ),
                total,
            )
        )
    if len(results) == 1:
        partial = results[0]
    else:
        order = plane ^ jnp.arange(planes, dtype=jnp.int32)
        partial = jnp.concatenate(results).reshape(planes, PLANE, cand_slots // 2, 2 * hist_rows)
        partial = partial[order].reshape(block_count, cand_slots // 2, 2 * hist_rows)
    gathered = lax.all_to_all(partial, "blk", split_axis=0, concat_axis=0, tiled=True)
    scores = call(
        finish_kernel,
        jax.ShapeDtypeStruct((cand_slots, hist_rows), jnp.float32),
        [gathered, cand_count.reshape(1, -1)],
    )
    return (item_out, scores.T)


def solution(mesh):
    in_specs = (
        P(("groups", "blk"), None),
        P("groups"),
        P(),
        P(),
        P(("groups", "blk"), None),
        P(),
        P(("groups", "blk"), None, None),
        P(("groups", "blk")),
        P(("groups", "blk"), None),
        P(("groups", "blk")),
    )
    out_specs = (P(("groups", "blk"), None), P(("groups", "blk"), None))
    return jax.shard_map(
        per_device, mesh=mesh, in_specs=in_specs, out_specs=out_specs, check_vma=False
    )
```
